256 devices in a mesh: layer: 32 (over x, y, core), tile: 8 (over z).
Axes of the slice: x: 4, y: 4, z: 8, core: 2. Of those that a mesh axis runs over, the one named last changes fastest.
Arguments:
- down_tiles: bfloat16 [32, 16, 3, 2, 512, 512], P('layer', 'tile'), may hold values from -0.109375 to 0.109375
- up_tiles: bfloat16 [32, 16, 3, 2, 512, 512], P('layer', 'tile'), may hold values from -0.109375 to 0.109375
- down_source: float32 [32, 2, 32, 8192], P('layer', None, None, 'tile'), may hold values from -3 to 3
- up_source: float32 [32, 2, 32, 8192], P('layer', None, None, 'tile'), may hold values from -3 to 3
- thickness: int32 [32], P('layer'), may hold values from 1 to 2
Outputs:
- field: float32 [32, 2, 32, 8192], P('layer', None, None, 'tile')
The draws below stay inside these ranges and needn't reach their ends.
All inputs are finite; a program needn't handle non-finite values.
Results may differ from the reference program's by a relative error of at most 0.04.
Values may be sent and summed in bfloat16 or wider, within the bound.
No kernel may reach another device: no remote copies, remote signals or barrier semaphores. Data moves between devices by JAX's collectives and lax.ppermute only.
A program may use at most 64 MiB of HBM per device.

```python
import jax
import jax.numpy as jnp
from jax import lax

TILE = 512
PTS = 8192
LAYERS = 32
BLOCKS = 16
ALLCOLS = 32


def with_ends(values, stream_key, smallest, largest):
    index_at = [jax.random.randint(jax.random.fold_in(stream_key, axis), (), 0, length) for axis, length in enumerate(values.shape)]
    main_axis = values.shape.index(max(values.shape))
    neighbour = index_at[:main_axis] + [(index_at[main_axis] + 1) % values.shape[main_axis]] + index_at[main_axis + 1:]
    return values.at[tuple(index_at)].set(smallest).at[tuple(neighbour)].set(largest)


def shard_levels(own_key, dims, split, least, top_value):
    def one(axis_at, parts):
        draws = jax.random.uniform(jax.random.fold_in(jax.random.fold_in(own_key, 6), axis_at), (parts,), jnp.float32, least / len(split), top_value / len(split))
        return jnp.repeat(jnp.exp(draws), dims[axis_at] // parts).reshape((-1,) + (1,) * (len(dims) - axis_at - 1))

    factor_of = one(*split[0])
    for cut in split[1:]:
        factor_of = factor_of * one(*cut)
    return factor_of


def normal_values(own_key, extent, deviation, reach, pieces=(), held_as=jnp.bfloat16):
    drawn = deviation * jax.random.normal(own_key, extent, jnp.float32)
    if pieces:
        drawn = drawn * shard_levels(own_key, extent, pieces, -0.22, 0.18)
    return jnp.clip(drawn, -reach, reach).astype(held_as)


def setup_inputs(seed: int = 0) -> dict:
    streams_of = jax.random.split(jax.random.key(seed), 6)
    return {
        "down_tiles": normal_values(streams_of[0], (LAYERS, BLOCKS, 3, 2, TILE, TILE), (6 * TILE) ** -0.5, 0.109375, ((0, 32), (1, 8))),
        "up_tiles": normal_values(streams_of[1], (LAYERS, BLOCKS, 3, 2, TILE, TILE), (6 * TILE) ** -0.5, 0.109375, ((0, 32), (1, 8))),
        "down_source": normal_values(streams_of[2], (LAYERS, 2, ALLCOLS, PTS), 0.5, 3.0, ((0, 32), (3, 8)), jnp.float32),
        "up_source": normal_values(streams_of[3], (LAYERS, 2, ALLCOLS, PTS), 0.5, 3.0, ((0, 32), (3, 8)), jnp.float32),
        "thickness": with_ends(jax.random.randint(streams_of[4], (LAYERS,), 1, 3), jax.random.fold_in(streams_of[4], 1), 1, 2).astype(jnp.int32),
    }


def apply_layer(layer_tiles, trace_in):
    columns = trace_in.shape[1]
    trace_in = lax.optimization_barrier(trace_in)
    blocks = trace_in.reshape(2, columns, BLOCKS, TILE).astype(jnp.float32)
    padded = jnp.pad(blocks, ((0, 0), (0, 0), (1, 1), (0, 0)))
    accum = jnp.zeros((2, 2, columns, BLOCKS, TILE), jnp.float32)
    for offset in range(3):
        window = padded[:, :, offset:offset + BLOCKS, :]
        accum = accum + jnp.einsum("pcbt,bqtu->pqcbu", window, layer_tiles[:, offset].astype(jnp.float32))
    real_part = accum[0, 0] - accum[1, 1]
    imag_part = accum[0, 1] + accum[1, 0]
    return jnp.stack([real_part, imag_part]).reshape(2, columns, PTS)


def transfer(layer_tiles, state_in, layer_thick):
    first_power = apply_layer(layer_tiles, state_in.astype(jnp.bfloat16))
    return lax.cond(layer_thick == 2,
                    lambda: apply_layer(layer_tiles, first_power.astype(jnp.bfloat16)),
                    lambda: first_power)


def sweep_step(state_in, layer_item):
    layer_tiles, source, layer_thick = layer_item
    updated = source + transfer(layer_tiles, state_in, layer_thick)
    return updated, updated


def reference(down_tiles, up_tiles, down_source, up_source, thickness):
    zeros_init = jnp.zeros((2, ALLCOLS, PTS), jnp.float32)
    _, downward = lax.scan(sweep_step, zeros_init, (down_tiles, down_source, thickness))
    _, upward = lax.scan(sweep_step, zeros_init, (up_tiles, up_source, thickness), reverse=True)
    return downward + upward
```

```python
import jax
import jax.numpy as jnp
from jax import lax
from jax.experimental import pallas as pl
from jax.experimental.pallas import tpu as pltpu
from jax.sharding import PartitionSpec as P

AXES = ("layer", "tile")


VMEM = pl.BlockSpec(memory_space=pltpu.VMEM)
ANY = pl.BlockSpec(memory_space=pl.ANY)
SMEM = pl.BlockSpec(memory_space=pltpu.SMEM)


def begin_kernel(info, own, down, up, other_down, other_up, partial, sides, centre, sems):
    slot, row, near_k, far_k = info[0], info[1], info[2], info[3]

    def fetch(source):
        pltpu.make_async_copy(source.at[1], centre, sems.at[0]).start()
        pltpu.make_async_copy(source.at[near_k], sides.at[0], sems.at[1]).start()
        pltpu.make_async_copy(source.at[far_k], sides.at[1], sems.at[2]).start()

    for index, source in enumerate((down.at[0, row], up.at[0, row], other_down.at[0], other_up.at[0])):
        @pl.when(slot == index)
        def _(source=source):
            fetch(source)

    pltpu.make_async_copy(other_down.at[0, 1], centre, sems.at[0]).wait()
    for part in range(2):
        partial[part] = jnp.dot(own[...], centre[part], preferred_element_type=jnp.float32)
    pltpu.make_async_copy(other_down.at[0, 0], sides.at[0], sems.at[1]).wait()
    pltpu.make_async_copy(other_down.at[0, 0], sides.at[1], sems.at[2]).wait()


def begin_apply(info, own, down, up, other_down, other_up):
    rows, width = own.shape
    moved = 6 * width * width * 2
    return pl.pallas_call(
        begin_kernel,
        out_shape=(
            jax.ShapeDtypeStruct((2, rows, width), jnp.float32),
            jax.ShapeDtypeStruct((2, 2, width, width), jnp.bfloat16),
        ),
        in_specs=[SMEM, VMEM, ANY, ANY, ANY, ANY],
        out_specs=(VMEM, VMEM),
        scratch_shapes=[
            pltpu.VMEM((2, width, width), jnp.bfloat16),
            pltpu.SemaphoreType.DMA((3,)),
        ],
        compiler_params=pltpu.CompilerParams(vmem_limit_bytes=8 << 20),
        cost_estimate=pl.CostEstimate(
            flops=4 * rows * width * width, bytes_accessed=moved, transcendentals=0
        ),
        name="begin_apply",
    )(info, own, down, up, other_down, other_up)


def end_kernel(info, near, far, partial, sides, source, new, value):
    columns = near.shape[0] // 2
    outer = jnp.where(info[5] == 1, far[...], jnp.zeros_like(far))
    parts = []
    for part in range(2):
        total = partial[part]
        total += jnp.dot(near[...], sides[0, part], preferred_element_type=jnp.float32)
        total += jnp.dot(outer, sides[1, part], preferred_element_type=jnp.float32)
        parts.append(total)
    real, imag = parts
    weight = info[4].astype(jnp.float32)
    for half, result in enumerate(
        (real[:columns] - imag[columns:], real[columns:] + imag[:columns])
    ):
        rows = pl.ds(half * columns, columns)
        result = result + weight * source[rows]
        value[rows] = result
        new[rows] = result.astype(new.dtype)


def end_apply(info, near, far, partial, sides, source):
    rows, width = near.shape
    return pl.pallas_call(
        end_kernel,
        out_shape=(
            jax.ShapeDtypeStruct((rows, width), jnp.bfloat16),
            jax.ShapeDtypeStruct((rows, width), jnp.float32),
        ),
        in_specs=[SMEM] + [VMEM] * 5,
        out_specs=(VMEM, VMEM),
        compiler_params=pltpu.CompilerParams(vmem_limit_bytes=8 << 20),
        cost_estimate=pl.CostEstimate(
            flops=8 * rows * width * width, bytes_accessed=8 * rows * width, transcendentals=0
        ),
        name="end_apply",
    )(info, near, far, partial, sides, source)


def shards(down_tiles, up_tiles, down_source, up_source, thickness):
    layers, tile_count = lax.axis_size("layer"), lax.axis_size("tile")
    chips = layers // 2
    layer, tile = lax.axis_index("layer"), lax.axis_index("tile")
    chip, core = layer // 2, layer % 2
    edge = (core + tile) % 2
    width = down_tiles.shape[-1]
    columns = down_source.shape[2]

    def at(chip_index, core_index, tile_index):
        return (2 * chip_index + core_index) * tile_count + tile_index

    def swaps(pairs):
        return [pair for a, b in pairs for pair in ((a, b), (b, a))]

    inside = swaps((at(i, 0, z), at(i, 1, z)) for i in range(chips) for z in range(tile_count))
    along = swaps(
        (at(i, (z + 1) % 2, z), at(i, (z + 1) % 2, z + 1))
        for i in range(chips)
        for z in range(tile_count - 1)
    )
    hops = [
        swaps(
            (at(i, c, z), at(i + 1, c, z))
            for i in range(start, chips - 1, 2)
            for c in range(2)
            for z in range(tile_count)
        )
        for start in range(2)
    ]

    def row(tiles, which):
        return lax.dynamic_index_in_dim(tiles[0], which, 0, True)

    def piece(source, which):
        cut = lax.dynamic_slice_in_dim(source[0], which * width, width, axis=2)
        return cut.reshape(1, 2 * columns, width)

    other_down = lax.ppermute(row(down_tiles, 1 - edge), AXES, inside)
    other_up = lax.ppermute(row(up_tiles, 1 - edge), AXES, inside)
    sent_source = jnp.concatenate([piece(down_source, 1 - edge), piece(up_source, 1 - edge)])
    sums = jnp.concatenate(
        [piece(down_source, edge), piece(up_source, edge), lax.ppermute(sent_source, AXES, inside)]
    )
    own_thick = thickness[0]
    other_thick = lax.ppermute(thickness, AXES, inside)[0]
    low_thick = jnp.where(core == 0, own_thick, other_thick)
    high_thick = jnp.where(core == 0, other_thick, own_thick)
    near_k, far_k = 2 - 2 * edge, 2 * edge
    has_far = jnp.where(edge == 0, tile > 0, tile < tile_count - 1).astype(jnp.int32)

    def slot_of(upward, place):
        position = jnp.where(upward, 1 - place, place)
        return upward.astype(jnp.int32) + 2 * (position != core).astype(jnp.int32)

    def one_step(step, state):
        trace, sums = state
        upward = (step < chips // 2) != (chip < chips // 2)
        live = (chip == step) | (chip == chips - 1 - step)
        sending = (chip == step - 1) | (chip == chips - step)
        taking = ((chip == step) & (chip > 0)) | (
            (chip == chips - 1 - step) & (chip < chips - 1)
        )
        hopping = sending | taking
        parity = (step + 1) % 2
        trace = lax.switch(
            jnp.where(hopping, 1 + parity, 0),
            [
                lambda t: t,
                lambda t: lax.ppermute(t, AXES, hops[0]),
                lambda t: lax.ppermute(t, AXES, hops[1]),
            ],
            trace,
        )
        first = jnp.where(upward, high_thick, low_thick)
        count = low_thick + high_thick
        begin = jnp.where(step == 0, first, 0)
        end = jnp.where(live, count, begin)

        def one_apply(index, state):
            trace, sums = state
            place = (index >= first).astype(jnp.int32)
            last = ((index == first - 1) | (index == count - 1)).astype(jnp.int32)
            slot = slot_of(upward, place)
            info = jnp.stack([slot, edge, near_k, far_k, last, has_far])
            near = lax.ppermute(trace, AXES, inside)
            far = lax.ppermute(trace, AXES, along)
            partial, sides = begin_apply(info, trace, down_tiles, up_tiles, other_down, other_up)
            source = lax.dynamic_index_in_dim(sums, slot, 0, False)
            new, value = end_apply(info, near, far, partial, sides, source)
            kept = jnp.where(last == 1, value, source)
            return new, lax.dynamic_update_index_in_dim(sums, kept, slot, 0)

        return lax.fori_loop(begin, end, one_apply, (trace, sums))

    begin_slot = slot_of(chip >= chips // 2, 0)
    trace = lax.dynamic_index_in_dim(sums, begin_slot, 0, False).astype(jnp.bfloat16)
    _, sums = lax.fori_loop(0, chips, one_step, (trace, sums))
    own_field = sums[0] + sums[1]
    other_field = lax.ppermute(sums[2] + sums[3], AXES, inside)
    left = jnp.where(edge == 0, own_field, other_field)
    right = jnp.where(edge == 0, other_field, own_field)
    return jnp.concatenate([left, right], axis=1).reshape(1, 2, columns, 2 * width)


def solution(mesh):
    return jax.shard_map(
        shards,
        mesh=mesh,
        in_specs=(
            P("layer", "tile", None, None, None, None),
            P("layer", "tile", None, None, None, None),
            P("layer", None, None, "tile"),
            P("layer", None, None, "tile"),
            P("layer"),
        ),
        out_specs=P("layer", None, None, "tile"),
        check_vma=False,
    )
```

```python
import jax
import jax.numpy as jnp
from jax import lax
from jax.experimental import pallas as pl
from jax.experimental.pallas import tpu as pltpu
from jax.sharding import PartitionSpec as P

AXES = ("layer", "tile")


VMEM = pl.BlockSpec(memory_space=pltpu.VMEM)
HBM = pl.BlockSpec(memory_space=pltpu.HBM)
SMEM = pl.BlockSpec(memory_space=pltpu.SMEM)


def pick_kernel(info, down, up, out, held, into, back):
    row = info[0]
    sources = [(d, k) for d in range(2) for k in range(3)]

    def arrive(n, d, k):
        source = (down, up)[d]
        return pltpu.make_async_copy(source.at[0, row, k], held.at[n], into.at[n])

    def leave(n, d, k):
        return pltpu.make_async_copy(held.at[n], out.at[d, k], back.at[n])

    for n, (d, k) in enumerate(sources):
        arrive(n, d, k).start()
    for n, (d, k) in enumerate(sources):
        arrive(n, d, k).wait()
        leave(n, d, k).start()
    for n, (d, k) in enumerate(sources):
        leave(n, d, k).wait()


def pick_rows(info, down, up):
    return pl.pallas_call(
        pick_kernel,
        out_shape=jax.ShapeDtypeStruct((2,) + down.shape[2:], down.dtype),
        in_specs=[SMEM, HBM, HBM],
        out_specs=HBM,
        scratch_shapes=[
            pltpu.VMEM((6,) + down.shape[3:], down.dtype),
            pltpu.SemaphoreType.DMA((6,)),
            pltpu.SemaphoreType.DMA((6,)),
        ],
        compiler_params=pltpu.CompilerParams(vmem_limit_bytes=12 << 20),
        name="pick_rows",
    )(info, down, up)


def begin_kernel(info, own, near, down, up, other, partial, last_tile, held, sems):
    slot, row, near_k, far_k = info[0], info[1], info[2], info[3]
    held_own, held_near = held.at[0], held.at[1]

    for index, source in enumerate((down.at[0, row], up.at[0, row], other.at[0], other.at[1])):

        @pl.when(slot == index)
        def _(source=source):
            pltpu.make_async_copy(source.at[1], held_own, sems.at[0]).start()
            pltpu.make_async_copy(source.at[near_k], held_near, sems.at[1]).start()
            pltpu.make_async_copy(source.at[far_k], last_tile, sems.at[2]).start()

    pltpu.make_async_copy(other.at[0, 1], held_own, sems.at[0]).wait()
    for part in range(2):
        partial[part] = jnp.dot(own[...], held[0, part], preferred_element_type=jnp.float32)
    pltpu.make_async_copy(other.at[0, 0], held_near, sems.at[1]).wait()
    for part in range(2):
        partial[part] += jnp.dot(near[...], held[1, part], preferred_element_type=jnp.float32)
    pltpu.make_async_copy(other.at[0, 0], last_tile, sems.at[2]).wait()


def begin_apply(info, own, near, down, up, other):
    rows, width = own.shape
    moved = 6 * width * width * 2
    return pl.pallas_call(
        begin_kernel,
        out_shape=(
            jax.ShapeDtypeStruct((2, rows, width), jnp.float32),
            jax.ShapeDtypeStruct((2, width, width), jnp.bfloat16),
        ),
        in_specs=[SMEM, VMEM, VMEM, HBM, HBM, HBM],
        out_specs=(VMEM, VMEM),
        scratch_shapes=[
            pltpu.VMEM((2, 2, width, width), jnp.bfloat16),
            pltpu.SemaphoreType.DMA((3,)),
        ],
        compiler_params=pltpu.CompilerParams(vmem_limit_bytes=8 << 20),
        cost_estimate=pl.CostEstimate(
            flops=8 * rows * width * width, bytes_accessed=moved, transcendentals=0
        ),
        name="begin_apply",
    )(info, own, near, down, up, other)


def end_kernel(info, far, partial, tile, source, new, value):
    columns = far.shape[0] // 2
    outer = jnp.where(info[5] == 1, far[...], jnp.zeros_like(far))
    real, imag = (
        partial[part] + jnp.dot(outer, tile[part], preferred_element_type=jnp.float32)
        for part in range(2)
    )
    weight = info[4].astype(jnp.float32)
    for half, result in enumerate(
        (real[:columns] - imag[columns:], real[columns:] + imag[:columns])
    ):
        rows = pl.ds(half * columns, columns)
        result = result + weight * source[rows]
        value[rows] = result
        new[rows] = result.astype(new.dtype)


def end_apply(info, far, partial, tile, source):
    rows, width = far.shape
    return pl.pallas_call(
        end_kernel,
        out_shape=(
            jax.ShapeDtypeStruct((rows, width), jnp.bfloat16),
            jax.ShapeDtypeStruct((rows, width), jnp.float32),
        ),
        in_specs=[SMEM] + [VMEM] * 4,
        out_specs=(VMEM, VMEM),
        compiler_params=pltpu.CompilerParams(vmem_limit_bytes=8 << 20),
        cost_estimate=pl.CostEstimate(
            flops=4 * rows * width * width, bytes_accessed=8 * rows * width, transcendentals=0
        ),
        name="end_apply",
    )(info, far, partial, tile, source)


def shards(down_tiles, up_tiles, down_source, up_source, thickness):
    layers, tile_count = lax.axis_size("layer"), lax.axis_size("tile")
    chips = layers // 2
    layer, tile = lax.axis_index("layer"), lax.axis_index("tile")
    chip, core = layer // 2, layer % 2
    edge = (core + tile + 1) % 2
    width = down_tiles.shape[-1]
    columns = down_source.shape[2]

    def at(chip_index, core_index, tile_index):
        return (2 * chip_index + core_index) * tile_count + tile_index

    def swaps(pairs):
        return [pair for a, b in pairs for pair in ((a, b), (b, a))]

    inside = swaps((at(i, 0, z), at(i, 1, z)) for i in range(chips) for z in range(tile_count))
    along = swaps(
        (at(i, z % 2, z), at(i, z % 2, z + 1))
        for i in range(chips)
        for z in range(tile_count - 1)
    )
    hops = [
        swaps(
            (at(i, c, z), at(i + 1, c, z))
            for i in range(start, chips - 1, 2)
            for c in range(2)
            for z in range(tile_count)
        )
        for start in range(2)
    ]

    def beyond(c, z):
        return z - 1 if (c + z) % 2 else z + 1

    corners = [
        swaps(
            (at(i, c, z), at(i + 1, c, beyond(c, z)))
            for i in range(start, chips - 1, 2)
            for c in range(2)
            for z in range(tile_count)
            if 0 <= beyond(c, z) < tile_count
        )
        for start in range(2)
    ]

    def piece(source, which):
        cut = lax.dynamic_slice_in_dim(source[0], which * width, width, axis=2)
        return cut.reshape(1, 2 * columns, width)

    sent_tiles = pick_rows((1 - edge).reshape(1), down_tiles, up_tiles)
    other_tiles = lax.ppermute(sent_tiles, AXES, inside)
    sent_source = jnp.concatenate([piece(down_source, 1 - edge), piece(up_source, 1 - edge)])
    sums = jnp.concatenate(
        [piece(down_source, edge), piece(up_source, edge), lax.ppermute(sent_source, AXES, inside)]
    )
    own_thick = thickness[0]
    other_thick = lax.ppermute(thickness, AXES, inside)[0]
    low_thick = jnp.where(core == 0, own_thick, other_thick)
    high_thick = jnp.where(core == 0, other_thick, own_thick)
    near_k, far_k = 2 - 2 * edge, 2 * edge
    has_far = jnp.where(edge == 0, tile > 0, tile < tile_count - 1).astype(jnp.int32)

    def slot_of(upward, place):
        position = jnp.where(upward, 1 - place, place)
        return upward.astype(jnp.int32) + 2 * (position != core).astype(jnp.int32)

    def one_step(step, state):
        upward = (step < chips // 2) != (chip < chips // 2)
        live = (chip == step) | (chip == chips - 1 - step)
        sending = (chip == step - 1) | (chip == chips - step)
        taking = ((chip == step) & (chip > 0)) | (
            (chip == chips - 1 - step) & (chip < chips - 1)
        )
        parity = (step + 1) % 2
        first = jnp.where(upward, high_thick, low_thick)
        count = low_thick + high_thick

        def apply(index, trace, far, sums, kept_if):
            place = (index >= first).astype(jnp.int32)
            last = kept_if & ((index == first - 1) | (index == count - 1))
            slot = slot_of(upward, place)
            info = jnp.stack([slot, edge, near_k, far_k, last.astype(jnp.int32), has_far])
            near = lax.ppermute(trace, AXES, inside)
            if far is None:
                far = lax.ppermute(trace, AXES, along)
            partial, tile = begin_apply(info, trace, near, down_tiles, up_tiles, other_tiles)
            source = lax.dynamic_index_in_dim(sums, slot, 0, False)
            new, value = end_apply(info, far, partial, tile, source)
            kept = jnp.where(last, value, source)
            return new, lax.dynamic_update_index_in_dim(sums, kept, slot, 0)

        def hop(start):
            def move(trace, sums):
                moved = lax.ppermute(trace, AXES, hops[start])
                corner = lax.ppermute(trace, AXES, corners[start])
                return apply(0, moved, corner, sums, taking)

            return move

        state = lax.switch(
            jnp.where(sending | taking, 1 + parity, 0),
            [lambda trace, sums: (trace, sums), hop(0), hop(1)],
            *state,
        )
        begin = jnp.where(taking, 1, first)
        end = jnp.where(live, count, begin)
        return lax.fori_loop(begin, end, lambda index, s: apply(index, s[0], None, s[1], live), state)

    begin_slot = slot_of(chip >= chips // 2, 0)
    trace = lax.dynamic_index_in_dim(sums, begin_slot, 0, False).astype(jnp.bfloat16)
    _, sums = lax.fori_loop(0, chips, one_step, (trace, sums))
    own_field = sums[0] + sums[1]
    other_field = lax.ppermute(sums[2] + sums[3], AXES, inside)
    left = jnp.where(edge == 0, own_field, other_field)
    right = jnp.where(edge == 0, other_field, own_field)
    return jnp.concatenate([left, right], axis=1).reshape(1, 2, columns, 2 * width)


def solution(mesh):
    return jax.shard_map(
        shards,
        mesh=mesh,
        in_specs=(
            P("layer", "tile", None, None, None, None),
            P("layer", "tile", None, None, None, None),
            P("layer", None, None, "tile"),
            P("layer", None, None, "tile"),
            P("layer"),
        ),
        out_specs=P("layer", None, None, "tile"),
        check_vma=False,
    )
```

```python
import functools

import jax
import jax.numpy as jnp
from jax import lax
from jax.experimental import pallas as pl
from jax.experimental.pallas import tpu as pltpu
from jax.sharding import PartitionSpec as P

AXES = ("layer", "tile")


VMEM = pl.BlockSpec(memory_space=pltpu.VMEM)
HBM = pl.BlockSpec(memory_space=pltpu.HBM)
SMEM = pl.BlockSpec(memory_space=pltpu.SMEM)


def pick_kernel(info, down, up, out, held, into, back):
    row = info[0]
    sources = [(d, k) for d in range(2) for k in range(3)]

    def arrive(n, d, k):
        source = (down, up)[d]
        return pltpu.make_async_copy(source.at[0, row, k], held.at[n], into.at[n])

    def leave(n, d, k):
        return pltpu.make_async_copy(held.at[n], out.at[d, k], back.at[n])

    for n, (d, k) in enumerate(sources):
        arrive(n, d, k).start()
    for n, (d, k) in enumerate(sources):
        arrive(n, d, k).wait()
        leave(n, d, k).start()
    for n, (d, k) in enumerate(sources):
        leave(n, d, k).wait()


def pick_rows(info, down, up):
    return pl.pallas_call(
        pick_kernel,
        out_shape=jax.ShapeDtypeStruct((2,) + down.shape[2:], down.dtype),
        in_specs=[SMEM, HBM, HBM],
        out_specs=HBM,
        scratch_shapes=[
            pltpu.VMEM((6,) + down.shape[3:], down.dtype),
            pltpu.SemaphoreType.DMA((6,)),
            pltpu.SemaphoreType.DMA((6,)),
        ],
        compiler_params=pltpu.CompilerParams(vmem_limit_bytes=12 << 20),
        name="pick_rows",
    )(info, down, up)


def begin_kernel(count, info, *refs):
    inputs, (down, up, other) = refs[:count], refs[count : count + 3]
    partial, left, held, sems = refs[count + 3 :]
    slot, row, near_k, far_k = info[0], info[1], info[2], info[3]
    places = [held.at[n] for n in range(count)] + [left.at[n] for n in range(3 - count)]

    for index, source in enumerate((down.at[0, row], up.at[0, row], other.at[0], other.at[1])):

        @pl.when(slot == index)
        def _(source=source):
            for n, k in enumerate((1, near_k, far_k)):
                pltpu.make_async_copy(source.at[k], places[n], sems.at[n]).start()

    for n in range(count):
        pltpu.make_async_copy(other.at[0, n], places[n], sems.at[n]).wait()
        for part in range(2):
            value = jnp.dot(inputs[n][...], held[n, part], preferred_element_type=jnp.float32)
            partial[part] = value if n == 0 else partial[part] + value
    for n in range(count, 3):
        pltpu.make_async_copy(other.at[0, n], places[n], sems.at[n]).wait()


def begin_apply(info, inputs, down, up, other):
    rows, width = inputs[0].shape
    count = len(inputs)
    return pl.pallas_call(
        functools.partial(begin_kernel, count),
        out_shape=(
            jax.ShapeDtypeStruct((2, rows, width), jnp.float32),
            jax.ShapeDtypeStruct((3 - count, 2, width, width), jnp.bfloat16),
        ),
        in_specs=[SMEM] + [VMEM] * count + [HBM] * 3,
        out_specs=(VMEM, VMEM),
        scratch_shapes=[
            pltpu.VMEM((count, 2, width, width), jnp.bfloat16),
            pltpu.SemaphoreType.DMA((3,)),
        ],
        compiler_params=pltpu.CompilerParams(vmem_limit_bytes=8 << 20),
        cost_estimate=pl.CostEstimate(
            flops=4 * count * rows * width * width,
            bytes_accessed=12 * width * width,
            transcendentals=0,
        ),
        name="begin_apply",
    )(info, *inputs, down, up, other)


def end_kernel(count, *refs):
    inputs, (partial, left, source, new, value) = refs[:count], refs[count:]
    columns = source.shape[0] // 2
    totals = []
    for part in range(2):
        total = partial[part]
        for n in range(count):
            total += jnp.dot(inputs[n][...], left[n, part], preferred_element_type=jnp.float32)
        totals.append(total)
    real, imag = totals
    for half, result in enumerate(
        (real[:columns] - imag[columns:], real[columns:] + imag[:columns])
    ):
        rows = pl.ds(half * columns, columns)
        result = result + source[rows]
        value[rows] = result
        new[rows] = result.astype(new.dtype)


def end_apply(inputs, partial, left, source):
    rows, width = source.shape
    count = len(inputs)
    return pl.pallas_call(
        functools.partial(end_kernel, count),
        out_shape=(
            jax.ShapeDtypeStruct((rows, width), jnp.bfloat16),
            jax.ShapeDtypeStruct((rows, width), jnp.float32),
        ),
        in_specs=[VMEM] * (count + 3),
        out_specs=(VMEM, VMEM),
        compiler_params=pltpu.CompilerParams(vmem_limit_bytes=8 << 20),
        cost_estimate=pl.CostEstimate(
            flops=4 * count * rows * width * width,
            bytes_accessed=8 * rows * width,
            transcendentals=0,
        ),
        name="end_apply",
    )(*inputs, partial, left, source)


def shards(down_tiles, up_tiles, down_source, up_source, thickness):
    layers, tile_count = lax.axis_size("layer"), lax.axis_size("tile")
    chips = layers // 2
    layer, tile = lax.axis_index("layer"), lax.axis_index("tile")
    chip, core = layer // 2, layer % 2
    half = tile_count // 2
    edge = jnp.where(tile < half, core, 1 - core)
    width = down_tiles.shape[-1]
    columns = down_source.shape[2]

    def at(chip_index, core_index, tile_index):
        return (2 * chip_index + core_index) * tile_count + tile_index

    def swaps(pairs):
        return [pair for a, b in pairs for pair in ((a, b), (b, a))]

    inside = swaps((at(i, 0, z), at(i, 1, z)) for i in range(chips) for z in range(tile_count))
    def side(c, z):
        return c if z < half else 1 - c

    def beyond(c, z):
        target = z + 1 if side(c, z) else z - 1
        if not 0 <= target < tile_count:
            return None
        return next(d for d in range(2) if side(d, target) != side(c, z)), target

    along = swaps(
        (at(i, c, z), at(i, *beyond(c, z)))
        for i in range(chips)
        for z in range(tile_count - 1)
        for c in range(2)
        if side(c, z)
    )
    hops = [
        swaps(
            (at(i, c, z), at(i + 1, c, z))
            for i in range(start, chips - 1, 2)
            for c in range(2)
            for z in range(tile_count)
        )
        for start in range(2)
    ]

    corners = [
        swaps(
            (at(i, c, z), at(i + 1, *beyond(c, z)))
            for i in range(start, chips - 1, 2)
            for c in range(2)
            for z in range(tile_count)
            if beyond(c, z)
        )
        for start in range(2)
    ]

    def piece(source, which):
        cut = lax.dynamic_slice_in_dim(source[0], which * width, width, axis=2)
        return cut.reshape(1, 2 * columns, width)

    sent_tiles = pick_rows((1 - edge).reshape(1), down_tiles, up_tiles)
    other_tiles = lax.ppermute(sent_tiles, AXES, inside)
    sent_source = jnp.concatenate([piece(down_source, 1 - edge), piece(up_source, 1 - edge)])
    sums = jnp.concatenate(
        [piece(down_source, edge), piece(up_source, edge), lax.ppermute(sent_source, AXES, inside)]
    )
    own_thick = thickness[0]
    other_thick = lax.ppermute(thickness, AXES, inside)[0]
    low_thick = jnp.where(core == 0, own_thick, other_thick)
    high_thick = jnp.where(core == 0, other_thick, own_thick)
    near_k, far_k = 2 - 2 * edge, 2 * edge

    def slot_of(upward, place):
        position = jnp.where(upward, 1 - place, place)
        return upward.astype(jnp.int32) + 2 * (position != core).astype(jnp.int32)

    def one_step(step, state):
        upward = (step < chips // 2) != (chip < chips // 2)
        live = (chip == step) | (chip == chips - 1 - step)
        sending = (chip == step - 1) | (chip == chips - step)
        taking = ((chip == step) & (chip > 0)) | (
            (chip == chips - 1 - step) & (chip < chips - 1)
        )
        parity = (step + 1) % 2
        first = jnp.where(upward, high_thick, low_thick)
        count = low_thick + high_thick

        def apply(index, trace, far, sums, kept_if):
            place = (index >= first).astype(jnp.int32)
            last = kept_if & ((index == first - 1) | (index == count - 1))
            slot = slot_of(upward, place)
            info = jnp.stack([slot, edge, near_k, far_k])
            if far is None:
                far = lax.ppermute(trace, AXES, along)
                near = lax.ppermute(trace, AXES, inside)
                early, late = [trace, near], [far]
            else:
                near = lax.ppermute(trace, AXES, inside)
                early, late = [trace], [near, far]
            partial, left = begin_apply(info, early, down_tiles, up_tiles, other_tiles)
            held = lax.dynamic_index_in_dim(sums, slot, 0, False)
            new, value = end_apply(late, partial, left, jnp.where(last, held, 0))
            kept = jnp.where(last, value, held)
            return new, lax.dynamic_update_index_in_dim(sums, kept, slot, 0)

        def hop(start):
            def move(trace, sums):
                moved = lax.ppermute(trace, AXES, hops[start])
                corner = lax.ppermute(trace, AXES, corners[start])
                return apply(0, moved, corner, sums, taking)

            return move

        state = lax.switch(
            jnp.where(sending | taking, 1 + parity, 0),
            [lambda trace, sums: (trace, sums), hop(0), hop(1)],
            *state,
        )
        begin = jnp.where(taking, 1, first)
        end = jnp.where(live, count, begin)
        return lax.fori_loop(begin, end, lambda index, s: apply(index, s[0], None, s[1], live), state)

    begin_slot = slot_of(chip >= chips // 2, 0)
    trace = lax.dynamic_index_in_dim(sums, begin_slot, 0, False).astype(jnp.bfloat16)
    _, sums = lax.fori_loop(0, chips, one_step, (trace, sums))
    own_field = sums[0] + sums[1]
    other_field = lax.ppermute(sums[2] + sums[3], AXES, inside)
    left = jnp.where(edge == 0, own_field, other_field)
    right = jnp.where(edge == 0, other_field, own_field)
    return jnp.concatenate([left, right], axis=1).reshape(1, 2, columns, 2 * width)


def solution(mesh):
    return jax.shard_map(
        shards,
        mesh=mesh,
        in_specs=(
            P("layer", "tile", None, None, None, None),
            P("layer", "tile", None, None, None, None),
            P("layer", None, None, "tile"),
            P("layer", None, None, "tile"),
            P("layer"),
        ),
        out_specs=P("layer", None, None, "tile"),
        check_vma=False,
    )
```

```python
import functools

import jax
import jax.numpy as jnp
from jax import lax
from jax.experimental import pallas as pl
from jax.experimental.pallas import tpu as pltpu
from jax.sharding import PartitionSpec as P

AXES = ("layer", "tile")


VMEM = pl.BlockSpec(memory_space=pltpu.VMEM)
HBM = pl.BlockSpec(memory_space=pltpu.HBM)
SMEM = pl.BlockSpec(memory_space=pltpu.SMEM)


def pick_kernel(info, down, up, out, held, into, back):
    row, upward = info[0], info[1]

    for index, source in enumerate((down, up)):

        @pl.when(upward == index)
        def _(source=source):
            for k in range(3):
                pltpu.make_async_copy(source.at[0, row, k], held.at[k], into.at[k]).start()

    for k in range(3):
        pltpu.make_async_copy(down.at[0, 0, k], held.at[k], into.at[k]).wait()
        pltpu.make_async_copy(held.at[k], out.at[k], back.at[k]).start()
    for k in range(3):
        pltpu.make_async_copy(held.at[k], out.at[k], back.at[k]).wait()


def pick_row(info, down, up):
    return pl.pallas_call(
        pick_kernel,
        out_shape=jax.ShapeDtypeStruct((4,) + down.shape[3:], down.dtype),
        in_specs=[SMEM, HBM, HBM],
        out_specs=HBM,
        scratch_shapes=[
            pltpu.VMEM((3,) + down.shape[3:], down.dtype),
            pltpu.SemaphoreType.DMA((3,)),
            pltpu.SemaphoreType.DMA((3,)),
        ],
        compiler_params=pltpu.CompilerParams(vmem_limit_bytes=8 << 20),
        name="pick_row",
    )(info, down, up)


def begin_kernel(count, info, *refs):
    inputs, (down, up, other, later) = refs[:count], refs[count : count + 4]
    partial, left, held, sems = refs[count + 4 :]
    slot, row, near_k, far_k = info[0], info[1], info[2], info[3]
    places = [held.at[n] for n in range(count)] + [left.at[n] for n in range(3 - count)]

    for index, source in enumerate((down.at[0, row], up.at[0, row], other, later)):

        @pl.when(slot == index)
        def _(source=source):
            for n, k in enumerate((1, near_k, far_k)):
                pltpu.make_async_copy(source.at[k], places[n], sems.at[n]).start()

    for n in range(count):
        pltpu.make_async_copy(other.at[n], places[n], sems.at[n]).wait()
        for part in range(2):
            value = jnp.dot(inputs[n][...], held[n, part], preferred_element_type=jnp.float32)
            partial[part] = value if n == 0 else partial[part] + value
    for n in range(count, 3):
        pltpu.make_async_copy(other.at[n], places[n], sems.at[n]).wait()


def begin_apply(info, inputs, tiles):
    rows, width = inputs[0].shape
    count = len(inputs)
    return pl.pallas_call(
        functools.partial(begin_kernel, count),
        out_shape=(
            jax.ShapeDtypeStruct((2, rows, width), jnp.float32),
            jax.ShapeDtypeStruct((3 - count, 2, width, width), jnp.bfloat16),
        ),
        in_specs=[SMEM] + [VMEM] * count + [HBM] * 4,
        out_specs=(VMEM, VMEM),
        scratch_shapes=[
            pltpu.VMEM((count, 2, width, width), jnp.bfloat16),
            pltpu.SemaphoreType.DMA((3,)),
        ],
        compiler_params=pltpu.CompilerParams(vmem_limit_bytes=8 << 20),
        cost_estimate=pl.CostEstimate(
            flops=4 * count * rows * width * width,
            bytes_accessed=12 * width * width,
            transcendentals=0,
        ),
        name="begin_apply",
    )(info, *inputs, *tiles)


def end_kernel(count, *refs):
    inputs, (partial, left, source, new, value) = refs[:count], refs[count:]
    columns = source.shape[0] // 2
    totals = []
    for part in range(2):
        total = partial[part]
        for n in range(count):
            total += jnp.dot(inputs[n][...], left[n, part], preferred_element_type=jnp.float32)
        totals.append(total)
    real, imag = totals
    for half, result in enumerate(
        (real[:columns] - imag[columns:], real[columns:] + imag[:columns])
    ):
        rows = pl.ds(half * columns, columns)
        result = result + source[rows]
        value[rows] = result
        new[rows] = result.astype(new.dtype)


def end_apply(inputs, partial, left, source):
    rows, width = source.shape
    count = len(inputs)
    return pl.pallas_call(
        functools.partial(end_kernel, count),
        out_shape=(
            jax.ShapeDtypeStruct((rows, width), jnp.bfloat16),
            jax.ShapeDtypeStruct((rows, width), jnp.float32),
        ),
        in_specs=[VMEM] * (count + 3),
        out_specs=(VMEM, VMEM),
        compiler_params=pltpu.CompilerParams(vmem_limit_bytes=8 << 20),
        cost_estimate=pl.CostEstimate(
            flops=4 * count * rows * width * width,
            bytes_accessed=8 * rows * width,
            transcendentals=0,
        ),
        name="end_apply",
    )(*inputs, partial, left, source)


def shards(down_tiles, up_tiles, down_source, up_source, thickness):
    layers, tile_count = lax.axis_size("layer"), lax.axis_size("tile")
    chips = layers // 2
    layer, tile = lax.axis_index("layer"), lax.axis_index("tile")
    chip, core = layer // 2, layer % 2
    half = tile_count // 2
    edge = jnp.where(tile < half, core, 1 - core)
    width = down_tiles.shape[-1]
    columns = down_source.shape[2]

    def at(chip_index, core_index, tile_index):
        return (2 * chip_index + core_index) * tile_count + tile_index

    def swaps(pairs):
        return [pair for a, b in pairs for pair in ((a, b), (b, a))]

    inside = swaps((at(i, 0, z), at(i, 1, z)) for i in range(chips) for z in range(tile_count))
    def side(c, z):
        return c if z < half else 1 - c

    def beyond(c, z):
        target = z + 1 if side(c, z) else z - 1
        if not 0 <= target < tile_count:
            return None
        return next(d for d in range(2) if side(d, target) != side(c, z)), target

    along = swaps(
        (at(i, c, z), at(i, *beyond(c, z)))
        for i in range(chips)
        for z in range(tile_count - 1)
        for c in range(2)
        if side(c, z)
    )
    hops = [
        swaps(
            (at(i, c, z), at(i + 1, c, z))
            for i in range(start, chips - 1, 2)
            for c in range(2)
            for z in range(tile_count)
        )
        for start in range(2)
    ]

    corners = [
        swaps(
            (at(i, c, z), at(i + 1, *beyond(c, z)))
            for i in range(start, chips - 1, 2)
            for c in range(2)
            for z in range(tile_count)
            if beyond(c, z)
        )
        for start in range(2)
    ]

    def piece(source, which):
        cut = lax.dynamic_slice_in_dim(source[0], which * width, width, axis=2)
        return cut.reshape(1, 2 * columns, width)

    firstly = (chip >= chips // 2).astype(jnp.int32)
    picks = [
        pick_row(jnp.stack([1 - edge, which]), down_tiles, up_tiles)
        for which in (firstly, 1 - firstly)
    ]
    early_tiles = lax.ppermute(picks[0], AXES, inside)
    sent_source = jnp.concatenate([piece(down_source, 1 - edge), piece(up_source, 1 - edge)])
    other_source = lax.ppermute(sent_source, AXES, inside)
    other_thick = lax.ppermute(thickness, AXES, inside)
    picked, early_tiles, other_source, other_thick = lax.optimization_barrier(
        (picks[1], early_tiles, other_source, other_thick)
    )
    others = (early_tiles, lax.ppermute(picked, AXES, inside))
    sums = jnp.concatenate([piece(down_source, edge), piece(up_source, edge), other_source])
    own_thick, other_thick = thickness[0], other_thick[0]
    low_thick = jnp.where(core == 0, own_thick, other_thick)
    high_thick = jnp.where(core == 0, other_thick, own_thick)
    near_k, far_k = 2 - 2 * edge, 2 * edge

    def slot_of(upward, place):
        position = jnp.where(upward, 1 - place, place)
        return upward.astype(jnp.int32) + 2 * (position != core).astype(jnp.int32)

    def apply(step, index, trace, far, sums, kept_if, others):
        upward = (step < chips // 2) != (chip < chips // 2)
        first = jnp.where(upward, high_thick, low_thick)
        place = (index >= first).astype(jnp.int32)
        last = kept_if & ((index == first - 1) | (index == low_thick + high_thick - 1))
        slot = slot_of(upward, place)
        second = jnp.asarray(step >= chips // 2).astype(jnp.int32)
        info = jnp.stack([jnp.where(slot < 2, slot, 2 + second), edge, near_k, far_k])
        if far is None:
            far = lax.ppermute(trace, AXES, along)
            near = lax.ppermute(trace, AXES, inside)
            early, late = [trace, near], [far]
        else:
            near = lax.ppermute(trace, AXES, inside)
            early, late = [trace], [near, far]
        partial, left = begin_apply(info, early, (down_tiles, up_tiles, *others))
        held = lax.dynamic_index_in_dim(sums, slot, 0, False)
        new, value = end_apply(late, partial, left, jnp.where(last, held, 0))
        kept = jnp.where(last, value, held)
        return new, lax.dynamic_update_index_in_dim(sums, kept, slot, 0)

    def one_step(step, state):
        upward = (step < chips // 2) != (chip < chips // 2)
        live = (chip == step) | (chip == chips - 1 - step)
        sending = (chip == step - 1) | (chip == chips - step)
        taking = ((chip == step) & (chip > 0)) | (
            (chip == chips - 1 - step) & (chip < chips - 1)
        )
        parity = (step + 1) % 2
        first = jnp.where(upward, high_thick, low_thick)
        count = low_thick + high_thick

        def hop(start):
            def move(trace, sums):
                moved = lax.ppermute(trace, AXES, hops[start])
                corner = lax.ppermute(trace, AXES, corners[start])
                return apply(step, 0, moved, corner, sums, taking, others)

            return move

        state = lax.switch(
            jnp.where(sending | taking, 1 + parity, 0),
            [lambda trace, sums: (trace, sums), hop(0), hop(1)],
            *state,
        )
        begin = jnp.where(taking, 1, first)
        end = jnp.where(live, count, begin)
        return lax.fori_loop(
            begin, end, lambda index, s: apply(step, index, s[0], None, s[1], live, others), state
        )

    begin_slot = slot_of(chip >= chips // 2, 0)
    trace = lax.dynamic_index_in_dim(sums, begin_slot, 0, False).astype(jnp.bfloat16)
    starting = (chip == 0) | (chip == chips - 1)
    begin = jnp.where(chip < chips // 2, low_thick, high_thick)
    state = lax.fori_loop(
        begin,
        jnp.where(starting, low_thick + high_thick, begin),
        lambda index, s: apply(0, index, s[0], None, s[1], starting, (others[0], others[0])),
        (trace, sums),
    )
    _, sums = lax.fori_loop(1, chips, one_step, state)
    own_field = sums[0] + sums[1]
    other_field = lax.ppermute(sums[2] + sums[3], AXES, inside)
    left = jnp.where(edge == 0, own_field, other_field)
    right = jnp.where(edge == 0, other_field, own_field)
    return jnp.concatenate([left, right], axis=1).reshape(1, 2, columns, 2 * width)


def solution(mesh):
    return jax.shard_map(
        shards,
        mesh=mesh,
        in_specs=(
            P("layer", "tile", None, None, None, None),
            P("layer", "tile", None, None, None, None),
            P("layer", None, None, "tile"),
            P("layer", None, None, "tile"),
            P("layer"),
        ),
        out_specs=P("layer", None, None, "tile"),
        check_vma=False,
    )
```

```python
import functools

import jax
import jax.numpy as jnp
from jax import lax
from jax.experimental import pallas as pl
from jax.experimental.pallas import tpu as pltpu
from jax.sharding import PartitionSpec as P

AXES = ("layer", "tile")


VMEM = pl.BlockSpec(memory_space=pltpu.VMEM)
HBM = pl.BlockSpec(memory_space=pltpu.HBM)
SMEM = pl.BlockSpec(memory_space=pltpu.SMEM)


def pick_kernel(info, down, up, out, held, into, back):
    row, upward = info[0], info[1]

    for index, source in enumerate((down, up)):

        @pl.when(upward == index)
        def _(source=source):
            for k in range(3):
                pltpu.make_async_copy(source.at[0, row, k], held.at[k], into.at[k]).start()

    for k in range(3):
        pltpu.make_async_copy(down.at[0, 0, k], held.at[k], into.at[k]).wait()
        pltpu.make_async_copy(held.at[k], out.at[k], back.at[k]).start()
    for k in range(3):
        pltpu.make_async_copy(held.at[k], out.at[k], back.at[k]).wait()


def pick_row(info, down, up, rows):
    return pl.pallas_call(
        pick_kernel,
        out_shape=jax.ShapeDtypeStruct((rows,) + down.shape[3:], down.dtype),
        in_specs=[SMEM, HBM, HBM],
        out_specs=HBM,
        scratch_shapes=[
            pltpu.VMEM((3,) + down.shape[3:], down.dtype),
            pltpu.SemaphoreType.DMA((3,)),
            pltpu.SemaphoreType.DMA((3,)),
        ],
        compiler_params=pltpu.CompilerParams(vmem_limit_bytes=8 << 20),
        name="pick_row",
    )(info, down, up)


def begin_kernel(count, info, *refs):
    inputs, (down, up, other, later) = refs[:count], refs[count : count + 4]
    partial, left, held, sems = refs[count + 4 :]
    slot, row, near_k, far_k = info[0], info[1], info[2], info[3]
    places = [held.at[n] for n in range(count)] + [left.at[n] for n in range(3 - count)]

    for index, source in enumerate((down.at[0, row], up.at[0, row], other, later)):

        @pl.when(slot == index)
        def _(source=source):
            for n, k in enumerate((1, near_k, far_k)):
                pltpu.make_async_copy(source.at[k], places[n], sems.at[n]).start()

    for n in range(count):
        pltpu.make_async_copy(other.at[n], places[n], sems.at[n]).wait()
        for part in range(2):
            value = jnp.dot(inputs[n][...], held[n, part], preferred_element_type=jnp.float32)
            partial[part] = value if n == 0 else partial[part] + value
    for n in range(count, 3):
        pltpu.make_async_copy(other.at[n], places[n], sems.at[n]).wait()


def begin_apply(info, inputs, tiles):
    rows, width = inputs[0].shape
    count = len(inputs)
    return pl.pallas_call(
        functools.partial(begin_kernel, count),
        out_shape=(
            jax.ShapeDtypeStruct((2, rows, width), jnp.float32),
            jax.ShapeDtypeStruct((3 - count, 2, width, width), jnp.bfloat16),
        ),
        in_specs=[SMEM] + [VMEM] * count + [HBM] * 4,
        out_specs=(VMEM, VMEM),
        scratch_shapes=[
            pltpu.VMEM((count, 2, width, width), jnp.bfloat16),
            pltpu.SemaphoreType.DMA((3,)),
        ],
        compiler_params=pltpu.CompilerParams(vmem_limit_bytes=8 << 20),
        cost_estimate=pl.CostEstimate(
            flops=4 * count * rows * width * width,
            bytes_accessed=12 * width * width,
            transcendentals=0,
        ),
        name="begin_apply",
    )(info, *inputs, *tiles)


def end_kernel(count, *refs):
    inputs, (partial, left, source, new, value) = refs[:count], refs[count:]
    columns = source.shape[0] // 2
    totals = []
    for part in range(2):
        total = partial[part]
        for n in range(count):
            total += jnp.dot(inputs[n][...], left[n, part], preferred_element_type=jnp.float32)
        totals.append(total)
    real, imag = totals
    for half, result in enumerate(
        (real[:columns] - imag[columns:], real[columns:] + imag[:columns])
    ):
        rows = pl.ds(half * columns, columns)
        result = result + source[rows]
        value[rows] = result
        new[rows] = result.astype(new.dtype)


def end_apply(inputs, partial, left, source):
    rows, width = source.shape
    count = len(inputs)
    return pl.pallas_call(
        functools.partial(end_kernel, count),
        out_shape=(
            jax.ShapeDtypeStruct((rows, width), jnp.bfloat16),
            jax.ShapeDtypeStruct((rows, width), jnp.float32),
        ),
        in_specs=[VMEM] * (count + 3),
        out_specs=(VMEM, VMEM),
        compiler_params=pltpu.CompilerParams(vmem_limit_bytes=8 << 20),
        cost_estimate=pl.CostEstimate(
            flops=4 * count * rows * width * width,
            bytes_accessed=8 * rows * width,
            transcendentals=0,
        ),
        name="end_apply",
    )(*inputs, partial, left, source)


def shards(down_tiles, up_tiles, down_source, up_source, thickness):
    layers, tile_count = lax.axis_size("layer"), lax.axis_size("tile")
    chips = layers // 2
    layer, tile = lax.axis_index("layer"), lax.axis_index("tile")
    chip, core = layer // 2, layer % 2
    half = tile_count // 2
    edge = jnp.where(tile < half, core, 1 - core)
    width = down_tiles.shape[-1]
    columns = down_source.shape[2]

    def at(chip_index, core_index, tile_index):
        return (2 * chip_index + core_index) * tile_count + tile_index

    def swaps(pairs):
        return [pair for a, b in pairs for pair in ((a, b), (b, a))]

    inside = swaps((at(i, 0, z), at(i, 1, z)) for i in range(chips) for z in range(tile_count))
    def side(c, z):
        return c if z < half else 1 - c

    def beyond(c, z):
        target = z + 1 if side(c, z) else z - 1
        if not 0 <= target < tile_count:
            return None
        return next(d for d in range(2) if side(d, target) != side(c, z)), target

    along = swaps(
        (at(i, c, z), at(i, *beyond(c, z)))
        for i in range(chips)
        for z in range(tile_count - 1)
        for c in range(2)
        if side(c, z)
    )
    hops = [
        swaps(
            (at(i, c, z), at(i + 1, c, z))
            for i in range(start, chips - 1, 2)
            for c in range(2)
            for z in range(tile_count)
        )
        for start in range(2)
    ]

    corners = [
        swaps(
            (at(i, c, z), at(i + 1, *beyond(c, z)))
            for i in range(start, chips - 1, 2)
            for c in range(2)
            for z in range(tile_count)
            if beyond(c, z)
        )
        for start in range(2)
    ]

    def piece(source, which):
        cut = lax.dynamic_slice_in_dim(source[0], which * width, width, axis=2)
        return cut.reshape(1, 2 * columns, width)

    firstly = (chip >= chips // 2).astype(jnp.int32)
    picks = [
        pick_row(jnp.stack([1 - edge, which]), down_tiles, up_tiles, rows)
        for which, rows in ((firstly, 3), (1 - firstly, 4))
    ]
    early_tiles = lax.ppermute(picks[0], AXES, inside)
    sent_source = jnp.concatenate([piece(down_source, 1 - edge), piece(up_source, 1 - edge)])
    other_source = lax.ppermute(sent_source, AXES, inside)
    other_thick = lax.ppermute(thickness, AXES, inside)
    picked, early_tiles, other_source, other_thick = lax.optimization_barrier(
        (picks[1], early_tiles, other_source, other_thick)
    )
    others = (early_tiles, lax.ppermute(picked, AXES, inside))
    sums = jnp.concatenate([piece(down_source, edge), piece(up_source, edge), other_source])
    own_thick, other_thick = thickness[0], other_thick[0]
    low_thick = jnp.where(core == 0, own_thick, other_thick)
    high_thick = jnp.where(core == 0, other_thick, own_thick)
    near_k, far_k = 2 - 2 * edge, 2 * edge

    def slot_of(upward, place):
        position = jnp.where(upward, 1 - place, place)
        return upward.astype(jnp.int32) + 2 * (position != core).astype(jnp.int32)

    def apply(step, index, trace, far, sums, kept_if, others):
        upward = (step < chips // 2) != (chip < chips // 2)
        first = jnp.where(upward, high_thick, low_thick)
        place = (index >= first).astype(jnp.int32)
        last = kept_if & ((index == first - 1) | (index == low_thick + high_thick - 1))
        slot = slot_of(upward, place)
        second = jnp.asarray(step >= chips // 2).astype(jnp.int32)
        info = jnp.stack([jnp.where(slot < 2, slot, 2 + second), edge, near_k, far_k])
        if far is None:
            far = lax.ppermute(trace, AXES, along)
            near = lax.ppermute(trace, AXES, inside)
            early, late = [trace, near], [far]
        else:
            near = lax.ppermute(trace, AXES, inside)
            early, late = [trace], [near, far]
        partial, left = begin_apply(info, early, (down_tiles, up_tiles, *others))
        held = lax.dynamic_index_in_dim(sums, slot, 0, False)
        new, value = end_apply(late, partial, left, jnp.where(last, held, 0))
        kept = jnp.where(last, value, held)
        return new, lax.dynamic_update_index_in_dim(sums, kept, slot, 0)

    def one_step(step, state):
        upward = (step < chips // 2) != (chip < chips // 2)
        live = (chip == step) | (chip == chips - 1 - step)
        sending = (chip == step - 1) | (chip == chips - step)
        taking = ((chip == step) & (chip > 0)) | (
            (chip == chips - 1 - step) & (chip < chips - 1)
        )
        parity = (step + 1) % 2
        first = jnp.where(upward, high_thick, low_thick)
        count = low_thick + high_thick

        def hop(start):
            def move(trace, sums):
                moved = lax.ppermute(trace, AXES, hops[start])
                corner = lax.ppermute(trace, AXES, corners[start])
                return apply(step, 0, moved, corner, sums, taking, others)

            return move

        state = lax.switch(
            jnp.where(sending | taking, 1 + parity, 0),
            [lambda trace, sums: (trace, sums), hop(0), hop(1)],
            *state,
        )
        begin = jnp.where(taking, 1, first)
        end = jnp.where(live, count, begin)
        return lax.fori_loop(
            begin, end, lambda index, s: apply(step, index, s[0], None, s[1], live, others), state
        )

    begin_slot = slot_of(chip >= chips // 2, 0)
    trace = lax.dynamic_index_in_dim(sums, begin_slot, 0, False).astype(jnp.bfloat16)
    starting = (chip == 0) | (chip == chips - 1)
    begin = jnp.where(chip < chips // 2, low_thick, high_thick)
    state = lax.fori_loop(
        begin,
        jnp.where(starting, low_thick + high_thick, begin),
        lambda index, s: apply(0, index, s[0], None, s[1], starting, (others[0], others[0])),
        (trace, sums),
    )
    _, sums = lax.fori_loop(1, chips, one_step, state)
    own_field = sums[0] + sums[1]
    other_field = lax.ppermute(sums[2] + sums[3], AXES, inside)
    left = jnp.where(edge == 0, own_field, other_field)
    right = jnp.where(edge == 0, other_field, own_field)
    return jnp.concatenate([left, right], axis=1).reshape(1, 2, columns, 2 * width)


def solution(mesh):
    return jax.shard_map(
        shards,
        mesh=mesh,
        in_specs=(
            P("layer", "tile", None, None, None, None),
            P("layer", "tile", None, None, None, None),
            P("layer", None, None, "tile"),
            P("layer", None, None, "tile"),
            P("layer"),
        ),
        out_specs=P("layer", None, None, "tile"),
        check_vma=False,
    )
```
